128 devices in a mesh: dp: 16 (over y, x_hi, core), tp: 8 (over z, x_lo).
Axes of the slice: x: 4 (x_hi: 2, x_lo: 2; x = x_hi * 2 + x_lo), y: 4, z: 4, core: 2. Of those that a mesh axis runs over, the one named last changes fastest.
Arguments:
- hidden_states: bfloat16 [16384, 3, 4096], P('dp', None, 'tp'), may hold values from -6 to 6
- fc_weight: bfloat16 [4096, 3, 4096], P('dp', None, 'tp'), may hold values from -0.0546875 to 0.0546875
- norm_gain: float32 [4096], replicated, may hold values from 0.1 to 1.9
- upstream: bfloat16 [16384, 4096], P(('dp', 'tp')), may hold values from -0.1875 to 0.1875
- lengths: int32 [128], P(('dp', 'tp')), may hold values from 1 to 128, as said below
Outputs:
- normed: bfloat16 [16384, 4096], P(('dp', 'tp'))
- grad_weight: float32 [4096, 3, 4096], P('dp', None, 'tp')
- grad_gain: float32 [4096], replicated
The draws below stay inside these ranges and needn't reach their ends.
Inputs may be any that keep to these rules, and one draw needn't show every extreme that they name: `lengths`: some sample carries loss at all 128 positions.
All inputs are finite; a program needn't handle non-finite values.
Results may differ from the reference program's by a relative error of at most 0.014.
Values may be sent and summed in bfloat16 or wider, within the bound.
No kernel may reach another device: no remote copies, remote signals or barrier semaphores. Data moves between devices by JAX's collectives and lax.ppermute only.
A program may use at most 128 MiB of HBM per device.

```python
import jax
import jax.numpy as jnp
from jax import lax

HIDDEN_SIZE = 4096
DRAFT = 4096
LAYERS = 3
TOK_DEV = 128
TOKENS = 16384
SAMPLES = 128
N_DP = 16
N_TP = 8


def draw_lengths(key, part):
    first_key = jax.random.fold_in(key, 11)
    second_key = jax.random.fold_in(key, 23)
    values = jax.random.randint(first_key, (SAMPLES,), 1, TOK_DEV + 1, dtype=jnp.int32)
    chosen = jax.random.randint(second_key, (), 0, SAMPLES, dtype=jnp.int32)
    return values.at[chosen].set(TOK_DEV)


def with_spikes(values, stream_key, source, target, parts, factor):
    owner, partner = [(jnp.arange(values.shape[position]) // (values.shape[position] // parts)).reshape([-1 if axis == position else 1 for axis in range(values.ndim)]) for position in (source, target)]
    chosen = jax.random.permutation(stream_key, parts)[partner]
    strong = (owner == chosen) | (owner == (partner + parts // 2) % parts)
    return jnp.where(strong, factor * values, values)


def block_levels(key, extent, cuts, least, top_value):
    gain, own = 1.0, jax.random.fold_in(key, 6)
    for position, blocks in cuts:
        steps = jnp.exp(jax.random.uniform(jax.random.fold_in(own, position), (blocks,), jnp.float32, least / len(cuts), top_value / len(cuts)))
        gain = gain * jnp.repeat(steps, extent[position] // blocks).reshape([-1 if axis == position else 1 for axis in range(len(extent))])
    return gain


def scatter_about(key, dims, spread, most, shards=(), kind=jnp.bfloat16):
    entries = spread * jax.random.normal(key, dims, jnp.float32)
    if shards:
        entries = entries * block_levels(key, dims, shards, -0.22, 0.18)
    return jnp.clip(entries, -most, most).astype(kind)


def heavy_noise(rng, shape, scale, bound, split, heavy, held_as=jnp.bfloat16):
    result = scale * jax.random.normal(rng, shape, jnp.float32)
    if split:
        result = result * block_levels(rng, shape, split, -0.22, 0.18)
    return jnp.clip(with_spikes(result, jax.random.fold_in(rng, 3), *heavy), -bound, bound).astype(held_as)


def setup_inputs(seed: int = 0) -> dict:
    key_of = jax.random.split(jax.random.key(seed), 6)
    hidden_states = scatter_about(key_of[0], (TOKENS, LAYERS, HIDDEN_SIZE), 1.0, 6.0, ((0, 16), (2, 8)))
    fc_weight = scatter_about(key_of[1], (DRAFT, LAYERS, HIDDEN_SIZE), (LAYERS * HIDDEN_SIZE) ** -0.5, 0.0546875, ((0, 16), (2, 8)))
    norm_gain = jnp.clip(1.0 + 0.18 * jax.random.normal(key_of[2], (DRAFT,), jnp.float32), 0.1, 1.9)
    upstream = heavy_noise(key_of[3], (TOKENS, DRAFT), TOKENS ** -0.5, 0.1875, ((0, 128),), (0, 1, 128, 5.5))
    lengths = draw_lengths(jax.random.fold_in(key_of[5], 71), 0)
    return {"hidden_states": hidden_states, "fc_weight": fc_weight, "norm_gain": norm_gain, "upstream": upstream, "lengths": lengths}


def round_trip(values):
    return lax.optimization_barrier(values.astype(jnp.bfloat16)).astype(jnp.float32)

def reference(hidden_states, fc_weight, norm_gain, upstream, lengths):
    tokens = hidden_states.shape[0]
    slab_width = HIDDEN_SIZE // N_TP
    merged = jnp.zeros((tokens, DRAFT), jnp.float32)
    for tp_index in range(N_TP):
        offset = tp_index * slab_width
        hidden_part = hidden_states[:, :, offset:offset + slab_width].reshape(tokens, LAYERS * slab_width)
        weight_part = fc_weight[:, :, offset:offset + slab_width].reshape(DRAFT, LAYERS * slab_width)
        product = lax.dot_general(hidden_part, weight_part, (((1,), (1,)), ((), ())), preferred_element_type=jnp.float32)
        merged = merged + round_trip(product)
    squares = lax.optimization_barrier(jnp.mean(merged * merged, axis=1, keepdims=True))
    inverse = lax.rsqrt(squares + 1e-05)
    scaled = merged * inverse
    normed = (scaled * norm_gain).astype(jnp.bfloat16)
    positions = jnp.arange(tokens, dtype=jnp.int32)
    owners = (positions // TOK_DEV).astype(jnp.int32)
    live_mask = (positions % TOK_DEV < lengths[owners]).astype(jnp.float32)
    incoming = upstream.astype(jnp.float32) * live_mask[:, None]
    grad_gain = lax.optimization_barrier(jnp.sum(incoming * scaled, axis=0))
    grad_scaled = incoming * norm_gain
    projection = lax.optimization_barrier(jnp.mean(grad_scaled * scaled, axis=1, keepdims=True))
    grad_merged = (inverse * (grad_scaled - scaled * projection)).astype(jnp.bfloat16)
    group_size = tokens // N_DP
    grad_weight = jnp.zeros((DRAFT, LAYERS * HIDDEN_SIZE), jnp.float32)
    for dp_index in range(N_DP):
        offset = dp_index * group_size
        grad_part = grad_merged[offset:offset + group_size]
        hidden_part = hidden_states[offset:offset + group_size].reshape(group_size, LAYERS * HIDDEN_SIZE)
        product = lax.dot_general(grad_part, hidden_part, (((0,), (0,)), ((), ())), preferred_element_type=jnp.float32)
        grad_weight = grad_weight + round_trip(product)
    return (normed, grad_weight.reshape(DRAFT, LAYERS, HIDDEN_SIZE), grad_gain)
```

```python
import functools

import jax
import jax.numpy as jnp
from jax import lax
from jax.experimental import pallas as pl
from jax.experimental.pallas import tpu as pltpu
from jax.sharding import PartitionSpec as P


RING = 4
F32 = jnp.float32
BF16 = jnp.bfloat16
NEAR = ((-1, 0), (1, 0), (0, 1), (0, 0))
FAR = ((2, 1), (-1, 1), (1, 1), (2, 0))


def place(index):
    d, t = index // 8, index % 8
    return {"y": d // 4, "xh": d // 2 % 2, "c": d % 2, "z": t // 2, "xl": t % 2}


def flat(p):
    return (p["y"] * 4 + p["xh"] * 2 + p["c"]) * 8 + p["z"] * 2 + p["xl"]


def moved(axis, size, step):
    pairs = []
    for source in range(128):
        p = place(source)
        p[axis] = (p[axis] + step) % size
        pairs.append((source, flat(p)))
    return pairs


def flipped(axis, mask):
    pairs = []
    for source in range(128):
        p = place(source)
        p[axis] ^= mask
        pairs.append((source, flat(p)))
    return pairs


PERMS = {
    "y+": moved("y", 4, 1),
    "y-": moved("y", 4, -1),
    "z+": moved("z", 4, 1),
    "z-": moved("z", 4, -1),
    "xh": flipped("xh", 1),
    "xl": flipped("xl", 1),
    "c": flipped("c", 1),
    "z1": flipped("z", 1),
    "z2": flipped("z", 2),
    "y1": flipped("y", 1),
    "y2": flipped("y", 2),
}


def send(value, way):
    return lax.ppermute(value, ("dp", "tp"), PERMS[way])


def halves(value):
    middle = value.shape[0] // 2
    return value[:middle], value[middle:]


def gather_near(own, ring, pair):
    from_prev = send(own, ring + "+")
    from_next = send(own, ring + "-")
    other = send(own, pair)
    return {(-1, 0): from_prev, (1, 0): from_next, (0, 1): other, (0, 0): own}


def gather_far(near, ring, pair):
    opposite = send(near[-1, 0], ring + "+")
    next_other = send(near[0, 1], ring + "-")
    prev_other = send(near[-1, 0], pair)
    low = send(halves(prev_other)[0], ring + "+")
    high = send(halves(next_other)[1], ring + "-")
    return {
        (2, 0): opposite,
        (1, 1): next_other,
        (-1, 1): prev_other,
        (2, 1): jnp.concatenate([low, high], axis=0),
    }


def add(*values):
    total = values[0].astype(F32)
    for value in values[1:]:
        total = total + value.astype(F32)
    return total


def scatter_far(far, ring, pair):
    low, high = halves(far[2, 1])
    low = send(low, ring + "-")
    high = send(high, ring + "+")
    to_prev = send(far[2, 0], ring + "-")
    prev_low, prev_high = halves(far[-1, 1])
    to_pair = send(
        jnp.concatenate([add(prev_low, low).astype(BF16), prev_high], axis=0), pair
    )
    next_low, next_high = halves(far[1, 1])
    to_next = send(
        jnp.concatenate([next_low, add(next_high, high).astype(BF16)], axis=0), ring + "+"
    )
    return to_prev, to_pair, to_next


def scatter_near(near, passed, ring, pair):
    to_prev, to_pair, to_next = passed
    from_prev = send(near[1, 0], ring + "+")
    other = send(add(near[0, 1], to_next).astype(BF16), pair)
    from_next = send(add(near[-1, 0], to_prev, to_pair).astype(BF16), ring + "-")
    return add(near[0, 0], from_prev, other, from_next)


def order_tokens_body(order, mine, theirs, out):
    @pl.when(pl.program_id(1) == 0)
    def _():
        out[...] = mine[...]

    @pl.when(pl.program_id(1) == 1)
    def _():
        out[...] = theirs[...]


def order_tokens(mine, theirs, order):
    layers, tokens, width = mine.shape
    block = tokens // 8
    source = pl.BlockSpec((layers, block, width), lambda i, j, order: (0, order[i], 0))
    return pl.pallas_call(
        order_tokens_body,
        out_shape=jax.ShapeDtypeStruct((layers, 2 * tokens, width), mine.dtype),
        grid_spec=pltpu.PrefetchScalarGridSpec(
            num_scalar_prefetch=1,
            grid=(8, 2),
            in_specs=[source, source],
            out_specs=pl.BlockSpec((layers, block, width), lambda i, j, order: (0, 2 * i + j, 0)),
        ),
        name="order_tokens",
    )(order, mine, theirs)


def order_columns_body(order, value, out):
    out[...] = value[...]


def order_columns(value, order):
    rows = value.shape[0]
    blocks = order.shape[0]
    return pl.pallas_call(
        order_columns_body,
        out_shape=jax.ShapeDtypeStruct((rows, blocks * 256), value.dtype),
        grid_spec=pltpu.PrefetchScalarGridSpec(
            num_scalar_prefetch=1,
            grid=(blocks,),
            in_specs=[pl.BlockSpec((rows, 256), lambda i, order: (0, order[i]))],
            out_specs=pl.BlockSpec((rows, 256), lambda i, order: (0, i)),
        ),
        name="order_columns",
    )(order, value)


def body(hidden_states, fc_weight, norm_gain, upstream, lengths):
    tok_dev, draft = upstream.shape
    slab = hidden_states.shape[2]
    shard = fc_weight.shape[0]
    dp, tp = lax.axis_index("dp"), lax.axis_index("tp")
    y, xh, core = dp // 4, dp // 2 % 2, dp % 2
    z, xl = tp // 2, tp % 2
    places = FAR + NEAR
    token_order = jnp.stack(
        [(z + r + RING) % RING * 2 + (xl + p) % 2 for r, p in places]
    ).astype(jnp.int32)
    chip_order = jnp.stack([(y + r + RING) % RING * 2 + (xh + p) % 2 for r, p in places])
    mine_order = (chip_order * 2 + core).astype(jnp.int32)
    sibling_order = (chip_order * 2 + 1 - core).astype(jnp.int32)

    weights = gather_near(fc_weight, "y", "xh")
    hidden = hidden_states.transpose(1, 0, 2)
    hidden_pair = send(hidden, "c")
    positions = lax.broadcasted_iota(jnp.int32, (tok_dev, 1), 0)
    masked = jnp.where(positions < lengths[0], upstream, jnp.zeros_like(upstream))
    masked = order_columns(masked, jnp.concatenate([mine_order, sibling_order]))
    incoming_pair = send(masked[:, draft // 2 :], "c")
    incoming = jnp.concatenate([masked[:, : draft // 2], incoming_pair], axis=0)
    gain = order_columns(norm_gain.reshape(1, draft), mine_order)
    tokens = order_tokens(hidden, hidden_pair, token_order)
    half = tokens.shape[1] // 2
    block = half // 4
    far_tokens, near_tokens = tokens[:, :half], tokens[:, half:]

    def project(weights, keys):
        piece = jnp.concatenate([weights[key] for key in keys], axis=0)
        outs = []
        for part in (far_tokens, near_tokens):
            outs.append(
                lax.dot_general(
                    part, piece, (((0, 2), (1, 2)), ((), ())), preferred_element_type=F32
                ).astype(BF16)
            )
        far = {key: outs[0][i * block : (i + 1) * block] for i, key in enumerate(FAR)}
        near = {key: outs[1][i * block : (i + 1) * block] for i, key in enumerate(NEAR)}
        return scatter_near(near, scatter_far(far, "z", "xl"), "z", "xl")

    merged_near = project(weights, NEAR)
    merged_far = project(gather_far(weights, "y", "xh"), FAR)
    merged = jnp.concatenate([merged_far, merged_near], axis=1)

    incoming = incoming.astype(F32)
    along = incoming * gain
    sums = jnp.concatenate(
        [
            jnp.sum(merged * merged, axis=1, keepdims=True),
            jnp.sum(along * merged, axis=1, keepdims=True),
        ],
        axis=1,
    )
    theirs = send(sums, "c")
    theirs = jnp.concatenate([theirs[tok_dev:], theirs[:tok_dev]], axis=0)
    sums = (sums + theirs) * (1.0 / draft)
    inverse = lax.rsqrt(sums[:, :1] + 1e-05)
    projection = inverse * sums[:, 1:]
    scaled = merged * inverse
    grad = (inverse * (along - scaled * projection)).astype(BF16)

    def differentiate(group):
        near = gather_near(group, "z", "xl")
        far = gather_far(near, "z", "xl")
        whole = jnp.concatenate([far[key] for key in FAR] + [near[key] for key in NEAR], axis=0)
        product = lax.dot_general(
            whole, tokens, (((0,), (1,)), ((), ())), preferred_element_type=F32
        ).astype(BF16)
        return [product[i * shard : (i + 1) * shard] for i in range(4)]

    far = dict(zip(FAR, differentiate(grad[:, : draft // 4])))
    passed = scatter_far(far, "y", "xh")
    near = dict(zip(NEAR, differentiate(grad[:, draft // 4 :])))
    grad_weight = scatter_near(near, passed, "y", "xh")

    normed = (scaled * gain).astype(BF16)
    normed_pair = send(normed[tok_dev:], "c")
    back = jnp.stack(
        [
            jnp.argmax(jnp.concatenate([mine_order, sibling_order]) == b)
            for b in range(16)
        ]
    ).astype(jnp.int32)
    normed = order_columns(
        jnp.concatenate([normed[:tok_dev], normed_pair], axis=1), back
    )
    total = jnp.sum(incoming * scaled, axis=0, keepdims=True)
    zero = jnp.zeros_like(total)
    total = order_columns(jnp.concatenate([total, zero], axis=1), back)
    total = total.reshape(32, draft // 32)
    for way in ("c", "xl", "xh", "z1", "z2", "y1", "y2"):
        total = total + send(total, way)
    return (normed, grad_weight, total.reshape(draft))


def solution(mesh):
    return jax.shard_map(
        body,
        mesh=mesh,
        in_specs=(
            P("dp", None, "tp"),
            P("dp", None, "tp"),
            P(),
            P(("dp", "tp"), None),
            P(("dp", "tp")),
        ),
        out_specs=(P(("dp", "tp"), None), P("dp", None, "tp"), P()),
        check_vma=False,
    )
```

```python
import jax
import jax.numpy as jnp
from jax import lax
from jax.experimental import pallas as pl
from jax.experimental.pallas import tpu as pltpu
from jax.sharding import PartitionSpec as P


RING = 4
F32 = jnp.float32
BF16 = jnp.bfloat16
NEAR = ((-1, 0), (1, 0), (0, 1), (0, 0))
FAR = ((2, 1), (-1, 1), (1, 1), (2, 0))
FIRST = ((2, 1), (2, 0), (1, 0), (1, 1))
SECOND = ((-1, 1), (-1, 0), (0, 1), (0, 0))


def place(index):
    d, t = index // 8, index % 8
    return {"y": d // 4, "xh": d // 2 % 2, "c": d % 2, "z": t // 2, "xl": t % 2}


def flat(p):
    return (p["y"] * 4 + p["xh"] * 2 + p["c"]) * 8 + p["z"] * 2 + p["xl"]


def moved(axis, size, step):
    pairs = []
    for source in range(128):
        p = place(source)
        p[axis] = (p[axis] + step) % size
        pairs.append((source, flat(p)))
    return pairs


def flipped(axis, mask):
    pairs = []
    for source in range(128):
        p = place(source)
        p[axis] ^= mask
        pairs.append((source, flat(p)))
    return pairs


PERMS = {
    "y+": moved("y", 4, 1),
    "y-": moved("y", 4, -1),
    "z+": moved("z", 4, 1),
    "z-": moved("z", 4, -1),
    "xh": flipped("xh", 1),
    "xl": flipped("xl", 1),
    "c": flipped("c", 1),
    "z1": flipped("z", 1),
    "z2": flipped("z", 2),
    "y1": flipped("y", 1),
    "y2": flipped("y", 2),
}


def send(value, way):
    return lax.ppermute(value, ("dp", "tp"), PERMS[way])


def halves(value):
    middle = value.shape[0] // 2
    return value[:middle], value[middle:]


def gather_near(own, ring, pair):
    from_prev = send(own, ring + "+")
    from_next = send(own, ring + "-")
    other = send(own, pair)
    return {(-1, 0): from_prev, (1, 0): from_next, (0, 1): other, (0, 0): own}


def gather_far(near, ring, pair):
    opposite = send(near[-1, 0], ring + "+")
    prev_other = send(near[-1, 0], pair)
    next_other = send(near[0, 1], ring + "-")
    low = send(halves(prev_other)[0], ring + "+")
    high = send(halves(next_other)[1], ring + "-")
    return {(2, 1): (low, high), (-1, 1): prev_other, (1, 1): next_other, (2, 0): opposite}


def add(*values):
    total = values[0].astype(F32)
    for value in values[1:]:
        total = total + value.astype(F32)
    return total


def add_half(whole, part, place):
    size = part.shape[0]
    widths = [(size * place, size * (1 - place), 0), (0, 0, 0)]
    return add(whole, lax.pad(part, jnp.zeros((), part.dtype), widths)).astype(BF16)


def scatter_start(far, ring):
    low, high = halves(far[2, 1])
    low = send(low, ring + "-")
    high = send(high, ring + "+")
    return low, high


def scatter_far(far, started, ring, pair):
    low, high = started
    to_prev = send(far[2, 0], ring + "-")
    to_pair = send(add_half(far[-1, 1], low, 0), pair)
    to_next = send(add_half(far[1, 1], high, 1), ring + "+")
    return to_prev, to_pair, to_next


def scatter_near(near, passed, ring, pair):
    to_prev, to_pair, to_next = passed
    from_prev = send(near[1, 0], ring + "+")
    other = send(add(near[0, 1], to_next).astype(BF16), pair)
    from_next = send(add(near[-1, 0], to_prev, to_pair).astype(BF16), ring + "-")
    return near[0, 0], from_prev, other, from_next


ANY = pl.BlockSpec(memory_space=pl.ANY)
VMEM = pl.BlockSpec(memory_space=pltpu.VMEM)
SMEM = pl.BlockSpec(memory_space=pltpu.SMEM)


def copy_all(copies):
    for copy in copies:
        copy.start()
    for copy in copies:
        copy.wait()


def project(weights, tokens, first, count):
    layers, _, width = tokens.shape
    depth = layers * width
    blocks = count // 256

    def kernel(*refs):
        sources, token_ref, outs = refs[: len(weights)], refs[len(weights)], refs[len(weights) + 1 : -6]
        w, x, staged, x_sems, w_sems, out_sems = refs[-6:]
        copies = []
        start = 0
        for source, piece in zip(sources, weights):
            done = 0
            while done < piece.shape[0]:
                layer, row = divmod(start, 256)
                size = min(256 - row, piece.shape[0] - done)
                block, layer = divmod(layer, layers)
                copies.append(
                    pltpu.make_async_copy(
                        source.at[pl.ds(done, size)],
                        w.at[pl.ds(block * 256 + row, size), pl.ds(layer * width, width)],
                        w_sems.at[len(copies)],
                    )
                )
                start += size
                done += size
        for copy in copies:
            copy.start()
        for i in range(blocks):
            for layer in range(layers):
                pltpu.make_async_copy(
                    token_ref.at[layer, pl.ds(first + i * 256, 256)],
                    x.at[i, :, pl.ds(layer * width, width)],
                    x_sems.at[i],
                ).start()
        for copy in copies:
            copy.wait()

        def block_step(i, carry):
            pltpu.make_async_copy(x.at[i], x.at[i], x_sems.at[i]).wait()
            staged[i] = lax.dot_general(
                x[i], w[...], (((1,), (1,)), ((), ())), preferred_element_type=F32
            ).astype(BF16)
            for k, out in enumerate(outs):

                @pl.when(i == k)
                def _():
                    pltpu.make_async_copy(staged.at[k], out, out_sems.at[k]).start()

            return carry

        lax.fori_loop(0, blocks, block_step, 0)
        for k, out in enumerate(outs):
            pltpu.make_async_copy(staged.at[k], out, out_sems.at[k]).wait()

    return pl.pallas_call(
        kernel,
        out_shape=(jax.ShapeDtypeStruct((256, 1024), BF16),) * blocks,
        in_specs=[ANY] * (len(weights) + 1),
        out_specs=(ANY,) * blocks,
        scratch_shapes=[
            pltpu.VMEM((1024, depth), BF16),
            pltpu.VMEM((blocks, 256, depth), BF16),
            pltpu.VMEM((blocks, 256, 1024), BF16),
            pltpu.SemaphoreType.DMA((blocks,)),
            pltpu.SemaphoreType.DMA((16,)),
            pltpu.SemaphoreType.DMA((blocks,)),
        ],
        compiler_params=pltpu.CompilerParams(vmem_limit_bytes=(8 + 2 * blocks) << 20),
        name="project",
    )(*weights, tokens)


def differentiate(pieces, tokens):
    layers, count, width = tokens.shape
    columns = pieces[0].shape[1]
    count_out = columns // 256
    chunk = {256: 1, 768: 3, 1024: 2}[columns]

    def kernel(*refs):
        sources, token_ref, outs = refs[: len(pieces)], refs[len(pieces)], refs[len(pieces) + 1 : -6]
        g, x, staged, x_sems, sems, out_sems = refs[-6:]
        copies = []
        start = 0
        for source, piece in zip(sources, pieces):
            size = piece.shape[0]
            copies.append(
                pltpu.make_async_copy(source, g.at[pl.ds(start, size)], sems.at[len(copies)])
            )
            start += size
        for copy in copies:
            copy.start()
        for i in range(layers):
            pltpu.make_async_copy(token_ref.at[i], x.at[i], x_sems.at[i]).start()
        for copy in copies:
            copy.wait()

        def write(i, j):
            return pltpu.make_async_copy(
                staged.at[i, j], outs[j].at[pl.ds(pl.multiple_of(i * 256, 256), 256)], out_sems.at[i, j]
            )

        def layer_step(i, carry):
            pltpu.make_async_copy(x.at[i], x.at[i], x_sems.at[i]).wait()

            def block_step(j, carry):
                size = chunk * 256
                product = lax.dot_general(
                    g[:, pl.ds(pl.multiple_of(j * size, size), size)],
                    x[i],
                    (((0,), (0,)), ((), ())),
                    preferred_element_type=F32,
                )
                staged[i, pl.ds(j * chunk, chunk)] = product.astype(BF16).reshape(chunk, 256, width)
                return carry

            lax.fori_loop(0, count_out // chunk, block_step, 0)
            for j in range(count_out):
                write(i, j).start()
            return carry

        lax.fori_loop(0, layers, layer_step, 0)
        for i in range(layers):
            for j in range(count_out):
                write(i, j).wait()

    return pl.pallas_call(
        kernel,
        out_shape=(jax.ShapeDtypeStruct((layers * 256, width), BF16),) * count_out,
        in_specs=[ANY] * (len(pieces) + 1),
        out_specs=(ANY,) * count_out,
        scratch_shapes=[
            pltpu.VMEM((count, columns), BF16),
            pltpu.VMEM((layers, count, width), BF16),
            pltpu.VMEM((layers, count_out, 256, width), BF16),
            pltpu.SemaphoreType.DMA((layers,)),
            pltpu.SemaphoreType.DMA((16,)),
            pltpu.SemaphoreType.DMA((layers, count_out)),
        ],
        compiler_params=pltpu.CompilerParams(vmem_limit_bytes=22 << 20),
        name="differentiate",
    )(*pieces, tokens)


def order_tokens(mine, theirs, order):
    layers, tokens, width = mine.shape
    block = tokens // 8

    def kernel(order, mine, theirs, out, sems):
        copy_all(
            [
                pltpu.make_async_copy(
                    source.at[:, pl.ds(pl.multiple_of(order[i] * block, block), block)],
                    out.at[:, pl.ds((2 * i + j) * block, block)],
                    sems.at[2 * i + j],
                )
                for i in range(8)
                for j, source in enumerate((mine, theirs))
            ]
        )

    return pl.pallas_call(
        kernel,
        out_shape=jax.ShapeDtypeStruct((layers, 2 * tokens, width), mine.dtype),
        in_specs=[SMEM, ANY, ANY],
        out_specs=VMEM,
        scratch_shapes=[pltpu.SemaphoreType.DMA((16,))],
        compiler_params=pltpu.CompilerParams(vmem_limit_bytes=8 << 20),
        name="order_tokens",
    )(order, mine, theirs)


def block_of(index):
    return pl.ds(index * 256 if isinstance(index, int) else pl.multiple_of(index * 256, 256), 256)


def gather_columns(order, value, gain):
    rows, width = value.shape

    def kernel(order, value, gain, mine, theirs, picked):
        for i in range(8):
            mine[:, block_of(i)] = value[:, block_of(order[i])]
            theirs[:, block_of(i)] = value[:, block_of(order[8 + i])]
            picked[:, block_of(i)] = gain[:, block_of(order[i])]

    return pl.pallas_call(
        kernel,
        out_shape=(
            jax.ShapeDtypeStruct((rows, width // 2), value.dtype),
            jax.ShapeDtypeStruct((rows, width // 2), value.dtype),
            jax.ShapeDtypeStruct((1, width // 2), gain.dtype),
        ),
        in_specs=[SMEM, VMEM, VMEM],
        out_specs=(VMEM, VMEM, VMEM),
        compiler_params=pltpu.CompilerParams(vmem_limit_bytes=6 << 20),
        name="gather_columns",
    )(order, value, gain)


def scatter_columns(order, mine, theirs):
    rows, width = mine.shape

    def kernel(order, mine, theirs, out):
        for i in range(8):
            out[:, block_of(order[i])] = mine[:, block_of(i)]
            out[:, block_of(order[8 + i])] = theirs[:, block_of(i)]

    return pl.pallas_call(
        kernel,
        out_shape=jax.ShapeDtypeStruct((rows, 2 * width), mine.dtype),
        in_specs=[SMEM, VMEM, VMEM],
        out_specs=VMEM,
        compiler_params=pltpu.CompilerParams(vmem_limit_bytes=6 << 20),
        name="scatter_columns",
    )(order, mine, theirs)


def listed(blocks, keys):
    pieces = []
    for key in keys:
        pieces.extend(blocks[key] if isinstance(blocks[key], tuple) else (blocks[key],))
    return pieces


def step(hidden_states, fc_weight, norm_gain, upstream, lengths):
    tok_dev, draft = upstream.shape
    shard, layers, slab = fc_weight.shape
    dp, tp = lax.axis_index("dp"), lax.axis_index("tp")
    core = dp % 2

    def chosen(places, ring_index, pair_index):
        ring = jnp.array([r % RING for r, _ in places], jnp.int32)
        pair = jnp.array([p for _, p in places], jnp.int32)
        return (ring_index + ring) % RING * 2 + (pair_index + pair) % 2

    token_order = chosen(FIRST + SECOND, tp // 2, tp)
    chip_order = chosen(FAR + NEAR, dp // 4, dp // 2)
    column_order = jnp.concatenate([chip_order * 2 + core, chip_order * 2 + 1 - core])

    hidden = hidden_states.transpose(1, 0, 2)
    hidden_pair = send(hidden, "c")
    own = fc_weight.transpose(1, 0, 2).reshape(layers * shard, slab)
    weights = gather_near(own, "y", "xh")
    positions = lax.broadcasted_iota(jnp.int32, (tok_dev, 1), 0)
    masked = jnp.where(positions < lengths[0], upstream, jnp.zeros_like(upstream))
    incoming, incoming_pair, gain = gather_columns(
        column_order, masked, norm_gain.reshape(1, draft)
    )
    incoming_pair = send(incoming_pair, "c")
    incoming = jnp.concatenate([incoming, incoming_pair], axis=0)
    tokens = order_tokens(hidden, hidden_pair, token_order)
    weights.update(gather_far(weights, "y", "xh"))
    merged = []
    for tag, keys in (("n", NEAR), ("f", FAR)):
        pieces = listed(weights, keys)
        if tag == "n":
            sums = dict(zip(FIRST, project(pieces, tokens, 0, 1024)))
            started = scatter_start(sums, "z")
            sums.update(zip(SECOND, project(pieces, tokens, 1024, 1024)))
        else:
            sums = dict(zip(FIRST + SECOND, project(pieces, tokens, 0, 2048)))
            started = scatter_start(sums, "z")
        passed = scatter_far(sums, started, "z", "xl")
        merged.append(add(*scatter_near(sums, passed, "z", "xl")))

    parts = []
    for source, begin, end in ((1, 0, 256), (1, 256, 1024), (0, 1024, 2048)):
        arriving = incoming[:, begin:end].astype(F32)
        scale = gain[:, begin:end]
        group = merged[source][:, begin % 1024 : begin % 1024 + end - begin]
        parts.append((group, arriving, arriving * scale, scale))
    sums = jnp.concatenate(
        [
            sum(jnp.sum(group * group, axis=1, keepdims=True) for group, _, _, _ in parts),
            sum(jnp.sum(along * group, axis=1, keepdims=True) for group, _, along, _ in parts),
        ],
        axis=1,
    )
    theirs = send(sums, "c")
    theirs = jnp.concatenate([theirs[tok_dev:], theirs[:tok_dev]], axis=0)
    sums = (sums + theirs) * (1.0 / draft)
    inverse = lax.rsqrt(sums[:, :1] + 1e-05)
    projection = inverse * sums[:, 1:]
    grads = [
        (inverse * (along - group * inverse * projection)).astype(BF16)
        for group, _, along, _ in parts
    ]

    gathered = []
    for grad, tag in zip(grads, "egh"):
        blocks = gather_near(grad, "z", "xl")
        blocks.update(gather_far(blocks, "z", "xl"))
        gathered.append(listed(blocks, FIRST + SECOND))
    sums = dict(zip(FAR[:1], differentiate(gathered[0], tokens)))
    started = scatter_start(sums, "y")
    sums.update(zip(FAR[1:], differentiate(gathered[1], tokens)))
    passed = scatter_far(sums, started, "y", "xh")
    sums.update(zip(NEAR, differentiate(gathered[2], tokens)))
    grad_weight = add(*scatter_near(sums, passed, "y", "xh")).reshape(layers, shard, slab)

    normed = jnp.concatenate(
        [(group * inverse * scale).astype(BF16) for group, _, _, scale in parts], axis=1
    )
    normed_pair = send(normed[tok_dev:], "c")
    normed = scatter_columns(column_order, normed[:tok_dev], normed_pair)
    total = jnp.concatenate(
        [
            jnp.sum(arriving * (group * inverse), axis=0, keepdims=True)
            for group, arriving, _, _ in parts
        ],
        axis=1,
    )
    total = scatter_columns(column_order, total, jnp.zeros_like(total))
    for way in ("xh", "y1", "y2", "xl", "z1", "z2", "c"):
        total = total + send(total, way)
    return (normed, grad_weight.transpose(1, 0, 2), total.reshape(draft))


def solution(mesh):
    return jax.shard_map(
        step,
        mesh=mesh,
        in_specs=(
            P("dp", None, "tp"),
            P("dp", None, "tp"),
            P(),
            P(("dp", "tp"), None),
            P(("dp", "tp")),
        ),
        out_specs=(P(("dp", "tp"), None), P("dp", None, "tp"), P()),
        check_vma=False,
    )
```

```python
import jax
import jax.numpy as jnp
from jax import lax
from jax.experimental import pallas as pl
from jax.experimental.pallas import tpu as pltpu
from jax.sharding import PartitionSpec as P


RING = 4
F32 = jnp.float32
BF16 = jnp.bfloat16
NEAR = ((-1, 0), (1, 0), (0, 1), (0, 0))
FAR = ((2, 1), (-1, 1), (1, 1), (2, 0))
FIRST = ((2, 1), (2, 0), (1, 0), (1, 1))
SECOND = ((-1, 1), (-1, 0), (0, 1), (0, 0))


def place(index):
    d, t = index // 8, index % 8
    return {"y": d // 4, "xh": d // 2 % 2, "c": d % 2, "z": t // 2, "xl": t % 2}


def flat(p):
    return (p["y"] * 4 + p["xh"] * 2 + p["c"]) * 8 + p["z"] * 2 + p["xl"]


def moved(axis, size, step):
    pairs = []
    for source in range(128):
        p = place(source)
        p[axis] = (p[axis] + step) % size
        pairs.append((source, flat(p)))
    return pairs


def flipped(axis, mask):
    pairs = []
    for source in range(128):
        p = place(source)
        p[axis] ^= mask
        pairs.append((source, flat(p)))
    return pairs


PERMS = {
    "y+": moved("y", 4, 1),
    "y-": moved("y", 4, -1),
    "z+": moved("z", 4, 1),
    "z-": moved("z", 4, -1),
    "xh": flipped("xh", 1),
    "xl": flipped("xl", 1),
    "c": flipped("c", 1),
    "z1": flipped("z", 1),
    "z2": flipped("z", 2),
    "y1": flipped("y", 1),
    "y2": flipped("y", 2),
}


def send(value, way):
    return lax.ppermute(value, ("dp", "tp"), PERMS[way])


def halves(value):
    middle = value.shape[0] // 2
    return value[:middle], value[middle:]


def gather_near(own, ring, pair):
    from_prev = send(own, ring + "+")
    from_next = send(own, ring + "-")
    other = send(own, pair)
    return {(-1, 0): from_prev, (1, 0): from_next, (0, 1): other, (0, 0): own}


def gather_far(near, ring, pair, whole=False):
    opposite = send(near[-1, 0], ring + "+")
    prev_other = send(near[-1, 0], pair)
    next_other = send(near[0, 1], ring + "-")
    if whole:
        last = send(prev_other, ring + "+")
    else:
        low = send(halves(prev_other)[0], ring + "+")
        high = send(halves(next_other)[1], ring + "-")
        last = (low, high)
    return {(2, 1): last, (-1, 1): prev_other, (1, 1): next_other, (2, 0): opposite}


def add(*values):
    total = values[0].astype(F32)
    for value in values[1:]:
        total = total + value.astype(F32)
    return total


def add_half(whole, part, place):
    size = part.shape[0]
    widths = [(size * place, size * (1 - place), 0), (0, 0, 0)]
    return add(whole, lax.pad(part, jnp.zeros((), part.dtype), widths)).astype(BF16)


def scatter_start(far, ring):
    low, high = halves(far[2, 1])
    low = send(low, ring + "-")
    high = send(high, ring + "+")
    return low, high


def scatter_far(far, started, ring, pair):
    low, high = started
    to_prev = send(far[2, 0], ring + "-")
    to_pair = send(add_half(far[-1, 1], low, 0), pair)
    to_next = send(add_half(far[1, 1], high, 1), ring + "+")
    return to_prev, to_pair, to_next


def scatter_near(near, passed, ring, pair):
    to_prev, to_pair, to_next = passed
    from_prev = send(near[1, 0], ring + "+")
    other = send(add(near[0, 1], to_next).astype(BF16), pair)
    from_next = send(add(near[-1, 0], to_prev, to_pair).astype(BF16), ring + "-")
    return near[0, 0], from_prev, other, from_next


ANY = pl.BlockSpec(memory_space=pl.ANY)
VMEM = pl.BlockSpec(memory_space=pltpu.VMEM)
SMEM = pl.BlockSpec(memory_space=pltpu.SMEM)


def copy_all(copies):
    for copy in copies:
        copy.start()
    for copy in copies:
        copy.wait()


def total_of(blocks):
    rows, width = blocks[0].shape

    def kernel(*refs):
        *sources, out = refs

        def step(i, carry):
            part = pl.ds(pl.multiple_of(i * 32, 32), 32)
            out[part] = add(*(source[part] for source in sources))
            return carry

        lax.fori_loop(0, rows // 32, step, 0)

    return pl.pallas_call(
        kernel,
        out_shape=jax.ShapeDtypeStruct((rows, width), F32),
        in_specs=[VMEM] * len(blocks),
        out_specs=VMEM,
        compiler_params=pltpu.CompilerParams(vmem_limit_bytes=8 << 20),
        name="total_of",
    )(*blocks)


def project(weights, tokens, first, count):
    layers, _, width = tokens.shape
    depth = layers * width
    blocks = count // 256

    def kernel(*refs):
        sources, token_ref, outs = refs[: len(weights)], refs[len(weights)], refs[len(weights) + 1 : -6]
        w, x, staged, x_sems, w_sems, out_sems = refs[-6:]
        copies = []
        start = 0
        for source, piece in zip(sources, weights):
            done = 0
            while done < piece.shape[0]:
                layer, row = divmod(start, 256)
                size = min(256 - row, piece.shape[0] - done)
                block, layer = divmod(layer, layers)
                copies.append(
                    pltpu.make_async_copy(
                        source.at[pl.ds(done, size)],
                        w.at[pl.ds(block * 256 + row, size), pl.ds(layer * width, width)],
                        w_sems.at[len(copies)],
                    )
                )
                start += size
                done += size
        for copy in copies:
            copy.start()
        for i in range(blocks):
            for layer in range(layers):
                pltpu.make_async_copy(
                    token_ref.at[layer, pl.ds(first + i * 256, 256)],
                    x.at[i, :, pl.ds(layer * width, width)],
                    x_sems.at[i],
                ).start()
        for copy in copies:
            copy.wait()

        def block_step(i, carry):
            pltpu.make_async_copy(x.at[i], x.at[i], x_sems.at[i]).wait()
            staged[i] = lax.dot_general(
                x[i], w[...], (((1,), (1,)), ((), ())), preferred_element_type=F32
            ).astype(BF16)
            for k, out in enumerate(outs):

                @pl.when(i == k)
                def _():
                    pltpu.make_async_copy(staged.at[k], out, out_sems.at[k]).start()

            return carry

        lax.fori_loop(0, blocks, block_step, 0)
        for k, out in enumerate(outs):
            pltpu.make_async_copy(staged.at[k], out, out_sems.at[k]).wait()

    return pl.pallas_call(
        kernel,
        out_shape=(jax.ShapeDtypeStruct((256, 1024), BF16),) * blocks,
        in_specs=[ANY] * (len(weights) + 1),
        out_specs=(ANY,) * blocks,
        scratch_shapes=[
            pltpu.VMEM((1024, depth), BF16),
            pltpu.VMEM((blocks, 256, depth), BF16),
            pltpu.VMEM((blocks, 256, 1024), BF16),
            pltpu.SemaphoreType.DMA((blocks,)),
            pltpu.SemaphoreType.DMA((16,)),
            pltpu.SemaphoreType.DMA((blocks,)),
        ],
        compiler_params=pltpu.CompilerParams(vmem_limit_bytes=(8 + 2 * blocks) << 20),
        name="project",
    )(*weights, tokens)


def differentiate(pieces, tokens):
    layers, count, width = tokens.shape
    columns = pieces[0].shape[1]
    count_out = columns // 256
    chunk = {256: 1, 768: 3, 1024: 2}[columns]

    def kernel(*refs):
        sources, token_ref, outs = refs[: len(pieces)], refs[len(pieces)], refs[len(pieces) + 1 : -6]
        g, x, staged, x_sems, sems, out_sems = refs[-6:]
        copies = []
        start = 0
        for source, piece in zip(sources, pieces):
            size = piece.shape[0]
            copies.append(
                pltpu.make_async_copy(source, g.at[pl.ds(start, size)], sems.at[len(copies)])
            )
            start += size
        for copy in copies:
            copy.start()
        for i in range(layers):
            pltpu.make_async_copy(token_ref.at[i], x.at[i], x_sems.at[i]).start()
        for copy in copies:
            copy.wait()

        def write(i, j):
            return pltpu.make_async_copy(
                staged.at[i, j], outs[j].at[pl.ds(pl.multiple_of(i * 256, 256), 256)], out_sems.at[i, j]
            )

        def layer_step(i, carry):
            pltpu.make_async_copy(x.at[i], x.at[i], x_sems.at[i]).wait()

            def block_step(j, carry):
                size = chunk * 256
                product = lax.dot_general(
                    g[:, pl.ds(pl.multiple_of(j * size, size), size)],
                    x[i],
                    (((0,), (0,)), ((), ())),
                    preferred_element_type=F32,
                )
                staged[i, pl.ds(j * chunk, chunk)] = product.astype(BF16).reshape(chunk, 256, width)
                return carry

            lax.fori_loop(0, count_out // chunk, block_step, 0)
            for j in range(count_out):
                write(i, j).start()
            return carry

        lax.fori_loop(0, layers, layer_step, 0)
        for i in range(layers):
            for j in range(count_out):
                write(i, j).wait()

    return pl.pallas_call(
        kernel,
        out_shape=(jax.ShapeDtypeStruct((layers * 256, width), BF16),) * count_out,
        in_specs=[ANY] * (len(pieces) + 1),
        out_specs=(ANY,) * count_out,
        scratch_shapes=[
            pltpu.VMEM((count, columns), BF16),
            pltpu.VMEM((layers, count, width), BF16),
            pltpu.VMEM((layers, count_out, 256, width), BF16),
            pltpu.SemaphoreType.DMA((layers,)),
            pltpu.SemaphoreType.DMA((16,)),
            pltpu.SemaphoreType.DMA((layers, count_out)),
        ],
        compiler_params=pltpu.CompilerParams(vmem_limit_bytes=22 << 20),
        name="differentiate",
    )(*pieces, tokens)


def order_tokens(mine, theirs, order):
    layers, tokens, width = mine.shape
    block = tokens // 8

    def kernel(order, mine, theirs, out, sems):
        copy_all(
            [
                pltpu.make_async_copy(
                    source.at[:, pl.ds(pl.multiple_of(order[i] * block, block), block)],
                    out.at[:, pl.ds((2 * i + j) * block, block)],
                    sems.at[2 * i + j],
                )
                for i in range(8)
                for j, source in enumerate((mine, theirs))
            ]
        )

    return pl.pallas_call(
        kernel,
        out_shape=jax.ShapeDtypeStruct((layers, 2 * tokens, width), mine.dtype),
        in_specs=[SMEM, ANY, ANY],
        out_specs=VMEM,
        scratch_shapes=[pltpu.SemaphoreType.DMA((16,))],
        compiler_params=pltpu.CompilerParams(vmem_limit_bytes=8 << 20),
        name="order_tokens",
    )(order, mine, theirs)


def block_of(index):
    return pl.ds(index * 256 if isinstance(index, int) else pl.multiple_of(index * 256, 256), 256)


def gather_columns(order, value, gain):
    rows, width = value.shape

    def kernel(order, value, gain, mine, theirs, picked):
        for i in range(8):
            mine[:, block_of(i)] = value[:, block_of(order[i])]
            theirs[:, block_of(i)] = value[:, block_of(order[8 + i])]
            picked[:, block_of(i)] = gain[:, block_of(order[i])]

    return pl.pallas_call(
        kernel,
        out_shape=(
            jax.ShapeDtypeStruct((rows, width // 2), value.dtype),
            jax.ShapeDtypeStruct((rows, width // 2), value.dtype),
            jax.ShapeDtypeStruct((1, width // 2), gain.dtype),
        ),
        in_specs=[SMEM, VMEM, VMEM],
        out_specs=(VMEM, VMEM, VMEM),
        compiler_params=pltpu.CompilerParams(vmem_limit_bytes=6 << 20),
        name="gather_columns",
    )(order, value, gain)


def scatter_columns(order, mine, theirs):
    rows, width = mine.shape

    def kernel(order, mine, theirs, out):
        for i in range(8):
            out[:, block_of(order[i])] = mine[:, block_of(i)]
            out[:, block_of(order[8 + i])] = theirs[:, block_of(i)]

    return pl.pallas_call(
        kernel,
        out_shape=jax.ShapeDtypeStruct((rows, 2 * width), mine.dtype),
        in_specs=[SMEM, VMEM, VMEM],
        out_specs=VMEM,
        compiler_params=pltpu.CompilerParams(vmem_limit_bytes=6 << 20),
        name="scatter_columns",
    )(order, mine, theirs)


def listed(blocks, keys):
    pieces = []
    for key in keys:
        pieces.extend(blocks[key] if isinstance(blocks[key], tuple) else (blocks[key],))
    return pieces


def step(hidden_states, fc_weight, norm_gain, upstream, lengths):
    tok_dev, draft = upstream.shape
    shard, layers, slab = fc_weight.shape
    dp, tp = lax.axis_index("dp"), lax.axis_index("tp")
    core = dp % 2

    def chosen(places, ring_index, pair_index):
        ring = jnp.array([r % RING for r, _ in places], jnp.int32)
        pair = jnp.array([p for _, p in places], jnp.int32)
        return (ring_index + ring) % RING * 2 + (pair_index + pair) % 2

    token_order = chosen(FIRST + SECOND, tp // 2, tp)
    chip_order = chosen(FAR + NEAR, dp // 4, dp // 2)
    column_order = jnp.concatenate([chip_order * 2 + core, chip_order * 2 + 1 - core])

    hidden = hidden_states.transpose(1, 0, 2)
    hidden_pair = send(hidden, "c")
    own = fc_weight.transpose(1, 0, 2).reshape(layers * shard, slab)
    weights = gather_near(own, "y", "xh")
    positions = lax.broadcasted_iota(jnp.int32, (tok_dev, 1), 0)
    masked = jnp.where(positions < lengths[0], upstream, jnp.zeros_like(upstream))
    incoming, incoming_pair, gain = gather_columns(
        column_order, masked, norm_gain.reshape(1, draft)
    )
    incoming_pair = send(incoming_pair, "c")
    incoming = jnp.concatenate([incoming, incoming_pair], axis=0)
    tokens = order_tokens(hidden, hidden_pair, token_order)
    weights.update(gather_far(weights, "y", "xh"))
    merged = []
    for tag, keys in (("n", NEAR), ("f", FAR)):
        pieces = listed(weights, keys)
        if tag == "n":
            sums = dict(zip(FIRST, project(pieces, tokens, 0, 1024)))
            started = scatter_start(sums, "z")
            sums.update(zip(SECOND, project(pieces, tokens, 1024, 1024)))
        else:
            sums = dict(zip(FIRST + SECOND, project(pieces, tokens, 0, 2048)))
            started = scatter_start(sums, "z")
        passed = scatter_far(sums, started, "z", "xl")
        merged.append(total_of(scatter_near(sums, passed, "z", "xl")))

    parts = []
    for source, begin, end in ((1, 0, 256), (1, 256, 1024), (0, 1024, 2048)):
        arriving = incoming[:, begin:end].astype(F32)
        scale = gain[:, begin:end]
        group = merged[source][:, begin % 1024 : begin % 1024 + end - begin]
        parts.append((group, arriving, arriving * scale, scale))
    sums = jnp.concatenate(
        [
            sum(jnp.sum(group * group, axis=1, keepdims=True) for group, _, _, _ in parts),
            sum(jnp.sum(along * group, axis=1, keepdims=True) for group, _, along, _ in parts),
        ],
        axis=1,
    )
    theirs = send(sums, "c")
    theirs = jnp.concatenate([theirs[tok_dev:], theirs[:tok_dev]], axis=0)
    sums = (sums + theirs) * (1.0 / draft)
    inverse = lax.rsqrt(sums[:, :1] + 1e-05)
    projection = inverse * sums[:, 1:]
    grads = [
        (inverse * (along - group * inverse * projection)).astype(BF16)
        for group, _, along, _ in parts
    ]

    gathered = []
    for grad, tag in zip(grads, "egh"):
        blocks = gather_near(grad, "z", "xl")
        blocks.update(gather_far(blocks, "z", "xl", tag == "e"))
        gathered.append(listed(blocks, FIRST + SECOND))
    sums = dict(zip(FAR[:1], differentiate(gathered[0], tokens)))
    started = scatter_start(sums, "y")
    sums.update(zip(FAR[1:], differentiate(gathered[1], tokens)))
    passed = scatter_far(sums, started, "y", "xh")
    sums.update(zip(NEAR, differentiate(gathered[2], tokens)))
    grad_weight = total_of(scatter_near(sums, passed, "y", "xh")).reshape(layers, shard, slab)

    normed = jnp.concatenate(
        [(group * inverse * scale).astype(BF16) for group, _, _, scale in parts], axis=1
    )
    normed_pair = send(normed[tok_dev:], "c")
    normed = scatter_columns(column_order, normed[:tok_dev], normed_pair)
    total = jnp.concatenate(
        [
            jnp.sum(arriving * (group * inverse), axis=0, keepdims=True)
            for group, arriving, _, _ in parts
        ],
        axis=1,
    )
    total = scatter_columns(column_order, total, jnp.zeros_like(total))
    for way in ("y1", "y2", "xh", "xl", "z1", "z2", "c"):
        total = total + send(total, way)
    return (normed, grad_weight.transpose(1, 0, 2), total.reshape(draft))


def solution(mesh):
    return jax.shard_map(
        step,
        mesh=mesh,
        in_specs=(
            P("dp", None, "tp"),
            P("dp", None, "tp"),
            P(),
            P(("dp", "tp"), None),
            P(("dp", "tp")),
        ),
        out_specs=(P(("dp", "tp"), None), P("dp", None, "tp"), P()),
        check_vma=False,
    )
```

```python
import jax
import jax.numpy as jnp
from jax import lax
from jax.experimental import pallas as pl
from jax.experimental.pallas import tpu as pltpu
from jax.sharding import PartitionSpec as P


RING = 4
F32 = jnp.float32
BF16 = jnp.bfloat16
NEAR = ((-1, 0), (1, 0), (0, 1), (0, 0))
FAR = ((2, 1), (-1, 1), (1, 1), (2, 0))
FIRST = ((2, 1), (2, 0), (1, 0))
SECOND = ((1, 1), (-1, 1), (-1, 0), (0, 1), (0, 0))


def place(index):
    d, t = index // 8, index % 8
    return {"y": d // 4, "xh": d // 2 % 2, "c": d % 2, "z": t // 2, "xl": t % 2}


def flat(p):
    return (p["y"] * 4 + p["xh"] * 2 + p["c"]) * 8 + p["z"] * 2 + p["xl"]


def moved(axis, size, step):
    pairs = []
    for source in range(128):
        p = place(source)
        p[axis] = (p[axis] + step) % size
        pairs.append((source, flat(p)))
    return pairs


def flipped(axis, mask):
    pairs = []
    for source in range(128):
        p = place(source)
        p[axis] ^= mask
        pairs.append((source, flat(p)))
    return pairs


PERMS = {
    "y+": moved("y", 4, 1),
    "y-": moved("y", 4, -1),
    "z+": moved("z", 4, 1),
    "z-": moved("z", 4, -1),
    "xh": flipped("xh", 1),
    "xl": flipped("xl", 1),
    "c": flipped("c", 1),
    "z1": flipped("z", 1),
    "z2": flipped("z", 2),
    "y1": flipped("y", 1),
    "y2": flipped("y", 2),
}


def send(value, way):
    return lax.ppermute(value, ("dp", "tp"), PERMS[way])


def halves(value):
    middle = value.shape[0] // 2
    return value[:middle], value[middle:]


def gather_near(own, ring, pair):
    from_prev = send(own, ring + "+")
    from_next = send(own, ring + "-")
    other = send(own, pair)
    return {(-1, 0): from_prev, (1, 0): from_next, (0, 1): other, (0, 0): own}


def gather_far(near, ring, pair, whole=False):
    opposite = send(near[-1, 0], ring + "+")
    prev_other = send(near[-1, 0], pair)
    next_other = send(near[0, 1], ring + "-")
    if whole:
        last = send(prev_other, ring + "+")
    else:
        low = send(halves(prev_other)[0], ring + "+")
        high = send(halves(next_other)[1], ring + "-")
        last = (low, high)
    return {(2, 1): last, (-1, 1): prev_other, (1, 1): next_other, (2, 0): opposite}


def add(*values):
    total = values[0].astype(F32)
    for value in values[1:]:
        total = total + value.astype(F32)
    return total


def add_half(whole, part, place):
    size = part.shape[0]
    widths = [(size * place, size * (1 - place), 0), (0, 0, 0)]
    return add(whole, lax.pad(part, jnp.zeros((), part.dtype), widths)).astype(BF16)


def scatter_start(far, ring):
    low, high = halves(far[2, 1])
    low = send(low, ring + "-")
    high = send(high, ring + "+")
    return low, high


def scatter_far(far, started, ring, pair):
    low, high = started
    to_prev = send(far[2, 0], ring + "-")
    to_pair = send(add_half(far[-1, 1], low, 0), pair)
    to_next = send(add_half(far[1, 1], high, 1), ring + "+")
    return to_prev, to_pair, to_next


def scatter_near(near, passed, ring, pair):
    to_prev, to_pair, to_next = passed
    from_prev = send(near[1, 0], ring + "+")
    other = send(add(near[0, 1], to_next).astype(BF16), pair)
    from_next = send(add(near[-1, 0], to_prev, to_pair).astype(BF16), ring + "-")
    return near[0, 0], from_prev, other, from_next


ANY = pl.BlockSpec(memory_space=pl.ANY)
VMEM = pl.BlockSpec(memory_space=pltpu.VMEM)
SMEM = pl.BlockSpec(memory_space=pltpu.SMEM)


def copy_all(copies):
    for copy in copies:
        copy.start()
    for copy in copies:
        copy.wait()


def total_of(blocks):
    rows, width = blocks[0].shape

    def kernel(*refs):
        *sources, out = refs

        def step(i, carry):
            part = pl.ds(pl.multiple_of(i * 32, 32), 32)
            out[part] = add(*(source[part] for source in sources))
            return carry

        lax.fori_loop(0, rows // 32, step, 0)

    return pl.pallas_call(
        kernel,
        out_shape=jax.ShapeDtypeStruct((rows, width), F32),
        in_specs=[VMEM] * len(blocks),
        out_specs=VMEM,
        compiler_params=pltpu.CompilerParams(vmem_limit_bytes=8 << 20),
        name="total_of",
    )(*blocks)


def project(weights, tokens, first, count):
    layers, _, width = tokens.shape
    depth = layers * width
    blocks = count // 256

    def kernel(*refs):
        sources, token_ref, outs = refs[: len(weights)], refs[len(weights)], refs[len(weights) + 1 : -6]
        w, x, staged, x_sems, w_sems, out_sems = refs[-6:]
        copies = []
        start = 0
        for source, piece in zip(sources, weights):
            done = 0
            while done < piece.shape[0]:
                layer, row = divmod(start, 256)
                size = min(256 - row, piece.shape[0] - done)
                block, layer = divmod(layer, layers)
                copies.append(
                    pltpu.make_async_copy(
                        source.at[pl.ds(done, size)],
                        w.at[pl.ds(block * 256 + row, size), pl.ds(layer * width, width)],
                        w_sems.at[len(copies)],
                    )
                )
                start += size
                done += size
        for copy in copies:
            copy.start()
        for i in range(blocks):
            for layer in range(layers):
                pltpu.make_async_copy(
                    token_ref.at[layer, pl.ds(first + i * 256, 256)],
                    x.at[i, :, pl.ds(layer * width, width)],
                    x_sems.at[i],
                ).start()
        for copy in copies:
            copy.wait()

        def block_step(i, carry):
            pltpu.make_async_copy(x.at[i], x.at[i], x_sems.at[i]).wait()
            staged[i] = lax.dot_general(
                x[i], w[...], (((1,), (1,)), ((), ())), preferred_element_type=F32
            ).astype(BF16)
            for k, out in enumerate(outs):

                @pl.when(i == k)
                def _():
                    pltpu.make_async_copy(staged.at[k], out, out_sems.at[k]).start()

            return carry

        lax.fori_loop(0, blocks, block_step, 0)
        for k, out in enumerate(outs):
            pltpu.make_async_copy(staged.at[k], out, out_sems.at[k]).wait()

    return pl.pallas_call(
        kernel,
        out_shape=(jax.ShapeDtypeStruct((256, 1024), BF16),) * blocks,
        in_specs=[ANY] * (len(weights) + 1),
        out_specs=(ANY,) * blocks,
        scratch_shapes=[
            pltpu.VMEM((1024, depth), BF16),
            pltpu.VMEM((blocks, 256, depth), BF16),
            pltpu.VMEM((blocks, 256, 1024), BF16),
            pltpu.SemaphoreType.DMA((blocks,)),
            pltpu.SemaphoreType.DMA((16,)),
            pltpu.SemaphoreType.DMA((blocks,)),
        ],
        compiler_params=pltpu.CompilerParams(vmem_limit_bytes=(8 + 2 * blocks) << 20),
        name="project",
    )(*weights, tokens)


def differentiate(pieces, tokens):
    layers, count, width = tokens.shape
    columns = pieces[0].shape[1]
    count_out = columns // 256
    chunk = {256: 1, 768: 3, 1024: 2}[columns]

    def kernel(*refs):
        sources, token_ref, outs = refs[: len(pieces)], refs[len(pieces)], refs[len(pieces) + 1 : -6]
        g, x, staged, x_sems, sems, out_sems = refs[-6:]
        copies = []
        start = 0
        for source, piece in zip(sources, pieces):
            size = piece.shape[0]
            copies.append(
                pltpu.make_async_copy(source, g.at[pl.ds(start, size)], sems.at[len(copies)])
            )
            start += size
        for copy in copies:
            copy.start()
        for i in range(layers):
            pltpu.make_async_copy(token_ref.at[i], x.at[i], x_sems.at[i]).start()
        for copy in copies:
            copy.wait()

        def write(i, j):
            return pltpu.make_async_copy(
                staged.at[i, j], outs[j].at[pl.ds(pl.multiple_of(i * 256, 256), 256)], out_sems.at[i, j]
            )

        def layer_step(i, carry):
            pltpu.make_async_copy(x.at[i], x.at[i], x_sems.at[i]).wait()

            def block_step(j, carry):
                size = chunk * 256
                product = lax.dot_general(
                    g[:, pl.ds(pl.multiple_of(j * size, size), size)],
                    x[i],
                    (((0,), (0,)), ((), ())),
                    preferred_element_type=F32,
                )
                staged[i, pl.ds(j * chunk, chunk)] = product.astype(BF16).reshape(chunk, 256, width)
                return carry

            lax.fori_loop(0, count_out // chunk, block_step, 0)
            for j in range(count_out):
                write(i, j).start()
            return carry

        lax.fori_loop(0, layers, layer_step, 0)
        for i in range(layers):
            for j in range(count_out):
                write(i, j).wait()

    return pl.pallas_call(
        kernel,
        out_shape=(jax.ShapeDtypeStruct((layers * 256, width), BF16),) * count_out,
        in_specs=[ANY] * (len(pieces) + 1),
        out_specs=(ANY,) * count_out,
        scratch_shapes=[
            pltpu.VMEM((count, columns), BF16),
            pltpu.VMEM((layers, count, width), BF16),
            pltpu.VMEM((layers, count_out, 256, width), BF16),
            pltpu.SemaphoreType.DMA((layers,)),
            pltpu.SemaphoreType.DMA((16,)),
            pltpu.SemaphoreType.DMA((layers, count_out)),
        ],
        compiler_params=pltpu.CompilerParams(vmem_limit_bytes=22 << 20),
        name="differentiate",
    )(*pieces, tokens)


def order_tokens(mine, theirs, order):
    layers, tokens, width = mine.shape
    block = tokens // 8

    def kernel(order, mine, theirs, out, sems):
        copy_all(
            [
                pltpu.make_async_copy(
                    source.at[:, pl.ds(pl.multiple_of(order[i] * block, block), block)],
                    out.at[:, pl.ds((2 * i + j) * block, block)],
                    sems.at[2 * i + j],
                )
                for i in range(8)
                for j, source in enumerate((mine, theirs))
            ]
        )

    return pl.pallas_call(
        kernel,
        out_shape=jax.ShapeDtypeStruct((layers, 2 * tokens, width), mine.dtype),
        in_specs=[SMEM, ANY, ANY],
        out_specs=VMEM,
        scratch_shapes=[pltpu.SemaphoreType.DMA((16,))],
        compiler_params=pltpu.CompilerParams(vmem_limit_bytes=8 << 20),
        name="order_tokens",
    )(order, mine, theirs)


def block_of(index):
    return pl.ds(index * 256 if isinstance(index, int) else pl.multiple_of(index * 256, 256), 256)


def gather_columns(order, value, gain):
    rows, width = value.shape

    def kernel(order, value, gain, mine, theirs, picked):
        for i in range(8):
            mine[:, block_of(i)] = value[:, block_of(order[i])]
            theirs[:, block_of(i)] = value[:, block_of(order[8 + i])]
            picked[:, block_of(i)] = gain[:, block_of(order[i])]

    return pl.pallas_call(
        kernel,
        out_shape=(
            jax.ShapeDtypeStruct((rows, width // 2), value.dtype),
            jax.ShapeDtypeStruct((rows, width // 2), value.dtype),
            jax.ShapeDtypeStruct((1, width // 2), gain.dtype),
        ),
        in_specs=[SMEM, VMEM, VMEM],
        out_specs=(VMEM, VMEM, VMEM),
        compiler_params=pltpu.CompilerParams(vmem_limit_bytes=6 << 20),
        name="gather_columns",
    )(order, value, gain)


def scatter_columns(order, mine, theirs):
    rows, width = mine.shape

    def kernel(order, mine, theirs, out):
        for i in range(8):
            out[:, block_of(order[i])] = mine[:, block_of(i)]
            out[:, block_of(order[8 + i])] = theirs[:, block_of(i)]

    return pl.pallas_call(
        kernel,
        out_shape=jax.ShapeDtypeStruct((rows, 2 * width), mine.dtype),
        in_specs=[SMEM, VMEM, VMEM],
        out_specs=VMEM,
        compiler_params=pltpu.CompilerParams(vmem_limit_bytes=6 << 20),
        name="scatter_columns",
    )(order, mine, theirs)


def listed(blocks, keys):
    pieces = []
    for key in keys:
        pieces.extend(blocks[key] if isinstance(blocks[key], tuple) else (blocks[key],))
    return pieces


def step(hidden_states, fc_weight, norm_gain, upstream, lengths):
    tok_dev, draft = upstream.shape
    shard, layers, slab = fc_weight.shape
    dp, tp = lax.axis_index("dp"), lax.axis_index("tp")
    core = dp % 2

    def chosen(places, ring_index, pair_index):
        ring = jnp.array([r % RING for r, _ in places], jnp.int32)
        pair = jnp.array([p for _, p in places], jnp.int32)
        return (ring_index + ring) % RING * 2 + (pair_index + pair) % 2

    token_order = chosen(FIRST + SECOND, tp // 2, tp)
    chip_order = chosen(FAR + NEAR, dp // 4, dp // 2)
    column_order = jnp.concatenate([chip_order * 2 + core, chip_order * 2 + 1 - core])

    hidden = hidden_states.transpose(1, 0, 2)
    hidden_pair = send(hidden, "c")
    own = fc_weight.transpose(1, 0, 2).reshape(layers * shard, slab)
    weights = gather_near(own, "y", "xh")
    positions = lax.broadcasted_iota(jnp.int32, (tok_dev, 1), 0)
    masked = jnp.where(positions < lengths[0], upstream, jnp.zeros_like(upstream))
    incoming, incoming_pair, gain = gather_columns(
        column_order, masked, norm_gain.reshape(1, draft)
    )
    incoming_pair = send(incoming_pair, "c")
    incoming = jnp.concatenate([incoming, incoming_pair], axis=0)
    tokens = order_tokens(hidden, hidden_pair, token_order)
    weights.update(gather_far(weights, "y", "xh"))
    merged = []
    for tag, keys in (("n", NEAR), ("f", FAR)):
        pieces = listed(weights, keys)
        if tag == "n":
            sums = dict(zip(FIRST, project(pieces, tokens, 0, 768)))
            started = scatter_start(sums, "z")
            sums.update(zip(SECOND, project(pieces, tokens, 768, 1280)))
        else:
            sums = dict(zip(FIRST + SECOND, project(pieces, tokens, 0, 2048)))
            started = scatter_start(sums, "z")
        passed = scatter_far(sums, started, "z", "xl")
        merged.append(total_of(scatter_near(sums, passed, "z", "xl")))

    parts = []
    for source, begin, end in ((1, 0, 256), (1, 256, 1024), (0, 1024, 2048)):
        arriving = incoming[:, begin:end].astype(F32)
        scale = gain[:, begin:end]
        group = merged[source][:, begin % 1024 : begin % 1024 + end - begin]
        parts.append((group, arriving, arriving * scale, scale))
    sums = jnp.concatenate(
        [
            sum(jnp.sum(group * group, axis=1, keepdims=True) for group, _, _, _ in parts),
            sum(jnp.sum(along * group, axis=1, keepdims=True) for group, _, along, _ in parts),
        ],
        axis=1,
    )
    theirs = send(sums, "c")
    theirs = jnp.concatenate([theirs[tok_dev:], theirs[:tok_dev]], axis=0)
    sums = (sums + theirs) * (1.0 / draft)
    inverse = lax.rsqrt(sums[:, :1] + 1e-05)
    projection = inverse * sums[:, 1:]
    grads = [
        (inverse * (along - group * inverse * projection)).astype(BF16)
        for group, _, along, _ in parts
    ]

    gathered = []
    for grad, tag in zip(grads, "egh"):
        blocks = gather_near(grad, "z", "xl")
        blocks.update(gather_far(blocks, "z", "xl", tag == "e"))
        gathered.append(listed(blocks, FIRST + SECOND))
    sums = dict(zip(FAR[:1], differentiate(gathered[0], tokens)))
    started = scatter_start(sums, "y")
    sums.update(zip(FAR[1:], differentiate(gathered[1], tokens)))
    passed = scatter_far(sums, started, "y", "xh")
    sums.update(zip(NEAR, differentiate(gathered[2], tokens)))
    grad_weight = total_of(scatter_near(sums, passed, "y", "xh")).reshape(layers, shard, slab)

    normed = jnp.concatenate(
        [(group * inverse * scale).astype(BF16) for group, _, _, scale in parts], axis=1
    )
    normed_pair = send(normed[tok_dev:], "c")
    normed = scatter_columns(column_order, normed[:tok_dev], normed_pair)
    total = jnp.concatenate(
        [
            jnp.sum(arriving * (group * inverse), axis=0, keepdims=True)
            for group, arriving, _, _ in parts
        ],
        axis=1,
    )
    total = scatter_columns(column_order, total, jnp.zeros_like(total))
    for way in ("y1", "y2", "xh", "xl", "z1", "z2", "c"):
        total = total + send(total, way)
    return (normed, grad_weight.transpose(1, 0, 2), total.reshape(draft))


def solution(mesh):
    return jax.shard_map(
        step,
        mesh=mesh,
        in_specs=(
            P("dp", None, "tp"),
            P("dp", None, "tp"),
            P(),
            P(("dp", "tp"), None),
            P(("dp", "tp")),
        ),
        out_specs=(P(("dp", "tp"), None), P("dp", None, "tp"), P()),
        check_vma=False,
    )
```
